32 devices in a mesh: groups: 2 (over y), ep: 4 (over z), sub: 2 (over x), tp: 2 (over core).
Axes of the slice: x: 2, y: 2, z: 4, core: 2. Of those that a mesh axis runs over, the one named last changes fastest.
Arguments:
- rows: bfloat16 [1024, 4096], P(('groups', 'ep'), ('sub', 'tp')), parts along dimension 0, may hold values from -6 to 6
- path: int32 [4, 1024, 1], P(None, ('groups', 'ep')), parts along dimension 1, may hold values from 0 to 7; in each aligned block of 128 rows (0 to 127, 128 to 255, ..., all dimensions but the last counted through in order) at most 32 rows name the same one
- norm_gain: float32 [8, 4096], P(('ep', 'tp')), may hold values from 0.1 to 1.9
- gate_weight: bfloat16 [8, 1408, 4096], P(('ep', 'tp'), 'sub'), may hold values from -0.09375 to 0.09375
- up_weight: bfloat16 [8, 1408, 4096], P(('ep', 'tp'), 'sub'), may hold values from -0.09375 to 0.09375
- down_weight: bfloat16 [8, 1408, 4096], P(('ep', 'tp'), 'sub'), may hold values from -0.15625 to 0.15625
Outputs:
- chained: bfloat16 [1024, 4096], P(('groups', 'ep'), ('sub', 'tp')), parts along dimension 0
The draws below stay inside these ranges and needn't reach their ends.
There are 2 independent parts, one for each index of `groups`. The reference program is written for one: setup_inputs(seed, part) draws one part's arguments, and reference() takes and returns one part's arrays. A program takes and returns all parts, laid end to end along the dimension named above; an argument that names none is the same for every part. Nothing has to cross between parts.
Inputs may be any that keep to these rules, and one draw needn't show every extreme that they name: `path`: in each aligned block of 128 rows of one hop no expert is named by more than 32 rows, and in some blocks one expert is named by exactly 32.
All inputs are finite; a program needn't handle non-finite values.
Results may differ from the reference program's by a relative error of at most 0.02.
Values may be sent and summed in bfloat16 or wider, within the bound.
No kernel may reach another device: no remote copies, remote signals or barrier semaphores. Data moves between devices by JAX's collectives and lax.ppermute only.
A program may use at most 64 MiB of HBM per device.

```python
import math
import jax
import jax.numpy as jnp
import numpy as np
from jax import lax

D = 4096
HID = 1408
HOPS = 4
ROWS_EP = 128
EXPERTS = 8
ROWS = 512
CAP = 32
HID_PARTS = 2


def block_scale(stream_key, dims, cuts, smallest, largest):
    level, own = 1.0, jax.random.fold_in(stream_key, 6)
    for position, parts in cuts:
        draws = jnp.exp(jax.random.uniform(jax.random.fold_in(own, position), (parts,), jnp.float32, smallest / len(cuts), largest / len(cuts)))
        level = level * jnp.repeat(draws, dims[position] // parts).reshape([-1 if axis == position else 1 for axis in range(len(dims))])
    return level


def shared_out(stream_key, own, number, rows, amount, top, most, lean):
    order = jax.random.permutation(stream_key, amount)
    crowded, common = portions_of(amount, rows * top, most, lean, True), portions_of(amount, rows * top, most, lean, False)
    places = jnp.arange(amount)

    def named(sizes, turn):
        used = int((sizes > 0).sum())
        fixed = max(1, used // 4)
        moved = fixed + (places - fixed + turn * (used - fixed)) % max(1, amount - fixed)
        return jnp.zeros((amount,), jnp.int32).at[order[jnp.where(places < fixed, places, moved)]].set(jnp.asarray(sizes, jnp.int32))

    sizes = jnp.where(number % 4 == 0, named(crowded, number // 4), named(common, number - number // 4 - 1))
    mixed = jax.random.permutation(jax.random.fold_in(own, 3), amount)
    source_of, receiver = mixed[0:amount // 2 * 2:2], mixed[1:amount // 2 * 2:2]
    room = jnp.minimum(sizes[source_of] - 1, most - sizes[receiver]) // 2
    room = jnp.where((source_of == order[0]) | (receiver == order[0]) | (sizes[receiver] == 0), 0, jnp.maximum(room, 0))
    moved = jax.random.randint(jax.random.fold_in(own, 4), (amount // 2,), 0, 1 << 20) % (room + 1)
    sizes = sizes.at[source_of].add(-moved).at[receiver].add(moved)
    items = jnp.searchsorted(jnp.cumsum(sizes), jnp.arange(rows * top), side="right").astype(jnp.int32)
    grid = items.reshape(top, rows).T
    grid = grid[jax.random.permutation(jax.random.fold_in(own, 1), rows)]
    turn = jax.random.randint(jax.random.fold_in(own, 2), (rows, 1), 0, top)
    return jnp.take_along_axis(grid, (jnp.arange(top)[None, :] + turn) % top, axis=1)


def portions_of(count, total, limit, skew, full):
    loads = [(1 << 20) // math.isqrt(rank ** skew) + 1 for rank in range(1, count + 1)]
    largest = limit if full else min(limit, max(-(-total // count), total * loads[0] // sum(loads)))
    least = 1 if total - largest >= count - 1 else 0
    holding, spare = [largest] + [least] * (count - 1), total - largest - least * (count - 1)
    while spare > 0:
        candidates = [i for i in range(1, count) if holding[i] < largest] or [i for i in range(1, count) if holding[i] < limit]
        pool, left = sum([loads[i] for i in candidates]), spare
        for i in candidates:
            extra = min(limit - holding[i], max(1, left * loads[i] // pool), spare)
            holding[i] = holding[i] + extra
            spare = spare - extra
    return np.array(holding)


def centred(rng, extent, deviation, most, shards=(), held_as=jnp.bfloat16):
    factor_of = block_scale(rng, extent, shards, -0.22, 0.18) if shards else 1.0
    entries = jax.random.normal(rng, extent, jnp.float32) * deviation * factor_of
    return jnp.minimum(jnp.maximum(entries, -most), most).astype(held_as)


def setup_inputs(seed: int = 0, part: int = 0) -> dict:
    arg_keys = jax.random.split(jax.random.key(seed), 7)
    part_splits = jax.random.split(jax.random.fold_in(arg_keys[6], part), 7)
    rows = centred(part_splits[0], (ROWS, D), 1.0, 6.0, ((0, 4), (1, 4)))
    path_keys = jax.random.split(jax.random.fold_in(part_splits[1], 1), HOPS * ROWS // ROWS_EP)
    path_turns = jax.random.permutation(jax.random.fold_in(part_splits[1], 3), HOPS * ROWS // ROWS_EP)
    path = jax.vmap(lambda own, number: shared_out(jax.random.fold_in(part_splits[1], 2), own, number, ROWS_EP, EXPERTS, 1, CAP, 2))(path_keys, path_turns).reshape((HOPS, ROWS, 1))
    norm_gain = jnp.clip(1.0 + 0.18 * jax.random.normal(arg_keys[2], (EXPERTS, D), jnp.float32), 0.1, 1.9)
    gate_weight = centred(arg_keys[3], (EXPERTS, HID, D), D ** -0.5, 0.09375, ((0, 8), (1, 2)))
    up_weight = centred(arg_keys[4], (EXPERTS, HID, D), D ** -0.5, 0.09375, ((0, 8), (1, 2)))
    down_weight = centred(arg_keys[5], (EXPERTS, HID, D), HID ** -0.5, 0.15625, ((0, 8), (1, 2)))
    return dict(rows=rows, path=path, norm_gain=norm_gain, gate_weight=gate_weight, up_weight=up_weight, down_weight=down_weight)


EPS = 1e-06

def one_expert(pieces):
    inputs, gain, gate_w, up_w, down_w = pieces
    values = inputs.astype(jnp.float32)
    meansq = lax.optimization_barrier(jnp.mean(values * values, axis=-1, keepdims=True))
    normed = (values * lax.rsqrt(meansq + EPS) * gain[None, :]).astype(jnp.bfloat16)
    gate = lax.dot_general(normed, gate_w, (((1,), (1,)), ((), ())), preferred_element_type=jnp.float32)
    upward = lax.dot_general(normed, up_w, (((1,), (1,)), ((), ())), preferred_element_type=jnp.float32)
    hidden = (jax.nn.silu(gate) * upward).astype(jnp.bfloat16)
    width = HID // HID_PARTS
    blocked = hidden.reshape(hidden.shape[0], HID_PARTS, width).astype(jnp.float32)
    downs = down_w.reshape(HID_PARTS, width, D).astype(jnp.float32)
    partials = jnp.einsum('rkh,khd->krd', blocked, downs).astype(jnp.bfloat16)
    partials = lax.optimization_barrier(partials).astype(jnp.float32)
    return lax.optimization_barrier(jnp.sum(partials, axis=0)).astype(jnp.bfloat16)

def hop_update(state, routing, norm_gain, gate_weight, up_weight, down_weight):
    blocks = state.shape[0] // ROWS_EP
    grouped = routing.reshape(blocks, ROWS_EP).astype(jnp.int32)
    onehot = (grouped[:, :, None] == jnp.arange(EXPERTS, dtype=jnp.int32)[None, None, :]).astype(jnp.int32)
    rank_in = lax.optimization_barrier(jnp.sum((jnp.cumsum(onehot, axis=1) - onehot) * onehot, axis=2)).astype(jnp.int32)
    block_index = jnp.arange(blocks, dtype=jnp.int32)[:, None]
    target = ((grouped * blocks + block_index) * CAP + rank_in).reshape(-1).astype(jnp.int32)
    buffer = jnp.zeros((EXPERTS * blocks * CAP, D), jnp.bfloat16).at[target].set(state)
    buffer = buffer.reshape(EXPERTS, blocks * CAP, D)
    updates = lax.map(one_expert, (buffer, norm_gain, gate_weight, up_weight, down_weight))
    update = updates.reshape(EXPERTS * blocks * CAP, D)[target]
    update = lax.optimization_barrier(update)
    return (state.astype(jnp.float32) + update.astype(jnp.float32)).astype(jnp.bfloat16)

def reference(rows, path, norm_gain, gate_weight, up_weight, down_weight):
    state = rows
    for hop_index in range(HOPS):
        state = hop_update(state, path[hop_index, :, 0], norm_gain, gate_weight, up_weight, down_weight)
    return state
```

```python
import functools

import jax
import jax.numpy as jnp
from jax import lax
from jax.experimental import pallas as pl
from jax.experimental.pallas import tpu as pltpu
from jax.sharding import PartitionSpec as P

EPS = 1e-06
BF16 = jnp.bfloat16
F32 = jnp.float32
VMEM = pl.BlockSpec(memory_space=pltpu.VMEM)
SMEM = pl.BlockSpec(memory_space=pltpu.SMEM)


def call(body, outs, *operands, scalars=0, limit=12 << 20, scratch=(), flops=0, name=None):
    specs = [SMEM] * scalars + [VMEM] * (len(operands) - scalars)
    moved = sum(o.size * o.dtype.itemsize for o in operands) + sum(
        o.size * o.dtype.itemsize for o in outs
    )
    return pl.pallas_call(
        body,
        out_shape=outs,
        in_specs=specs,
        out_specs=[VMEM] * len(outs),
        scratch_shapes=list(scratch),
        compiler_params=pltpu.CompilerParams(vmem_limit_bytes=limit),
        cost_estimate=pl.CostEstimate(flops=flops, bytes_accessed=moved, transcendentals=0),
        name=name,
    )(*operands)


def swap(value, axis, step):
    return lax.ppermute(value, axis, [(i, i ^ step) for i in range(lax.axis_size(axis))])


def route_body(tp_count, capacity, relative, place_ref, path_ref, mine_ref, other_ref, pick_ref):
    ep_index, core_index = place_ref[0], place_ref[2]
    hops, local_rows, _ = path_ref.shape
    slots = mine_ref.shape[2]
    lane = lax.broadcasted_iota(jnp.int32, (local_rows, slots), 1)
    row = lax.broadcasted_iota(jnp.int32, (local_rows, local_rows), 0)
    col = lax.broadcasted_iota(jnp.int32, (local_rows, local_rows), 1)
    earlier = (col < row).astype(BF16)
    for hop in range(hops):
        expert = path_ref[hop]
        onehot = (expert == lane).astype(F32)
        before = jnp.dot(earlier, onehot.astype(BF16), preferred_element_type=F32)
        rank = jnp.sum(before * onehot, axis=1, keepdims=True).astype(jnp.int32)
        dest, core = lax.div(expert, tp_count), lax.rem(expert, tp_count)
        if relative:
            dest = lax.bitwise_xor(dest, ep_index)
        target = dest * capacity + rank
        here = jnp.where(core == core_index, target, -1) == lane
        there = jnp.where(core == core_index, -1, target) == lane
        mine_ref[hop] = here.astype(BF16)
        other_ref[hop] = there.astype(BF16)
        pick_ref[hop] = here.astype(F32).T.astype(BF16)


def first_body(width, place_ref, own_ref, far_ref, pick_ref, state_ref, *piece_refs):
    core = place_ref[2]
    state_ref[:, pl.ds(pl.multiple_of(core * width, width), width)] = own_ref[...]
    state_ref[:, pl.ds(pl.multiple_of((1 - core) * width, width), width)] = far_ref[...]
    pack(state_ref[...], pick_ref[...], piece_refs)


def pack(state, pick, piece_refs):
    height = piece_refs[0].shape[0]
    packed = jnp.dot(pick, state, preferred_element_type=F32).astype(BF16)
    for s, ref in enumerate(piece_refs):
        ref[...] = packed[s * height : (s + 1) * height]


def expert_body(count, sub_count, place_ref, *refs):
    x = place_ref[1]
    data = refs[: count * sub_count]
    gain_ref, gate_ref, up_ref, down_ref = refs[count * sub_count : count * sub_count + 4]
    out_refs = refs[count * sub_count + 4 :]
    width = data[0].shape[1]
    capacity = data[0].shape[0]
    total = 0.0
    values = []
    for u in range(sub_count):
        part = jnp.concatenate([data[i * sub_count + u][...] for i in range(count)], axis=0)
        part = part.astype(F32)
        values.append(part)
        total = total + jnp.sum(part * part, axis=-1, keepdims=True)
    scale = lax.rsqrt(total / (width * sub_count) + EPS)
    gate = up = 0.0
    dims = (((1,), (1,)), ((), ()))
    for u in range(sub_count):
        columns = pl.ds(pl.multiple_of(lax.bitwise_xor(x, u) * width, width), width)
        normed = (values[u] * scale * gain_ref[:, columns]).astype(BF16)
        gate = gate + lax.dot_general(normed, gate_ref[:, columns], dims, preferred_element_type=F32)
        up = up + lax.dot_general(normed, up_ref[:, columns], dims, preferred_element_type=F32)
    hidden = (gate / (1.0 + jnp.exp(-gate)) * up).astype(BF16)
    for u in range(sub_count):
        columns = pl.ds(pl.multiple_of(lax.bitwise_xor(x, u) * width, width), width)
        partial = jnp.dot(hidden, down_ref[:, columns], preferred_element_type=F32).astype(BF16)
        for i in range(count):
            out_refs[i * sub_count + u][...] = partial[i * capacity : (i + 1) * capacity]


def sum_body(*refs):
    total = refs[0][...].astype(F32)
    for ref in refs[1:-1]:
        total = total + ref[...].astype(F32)
    refs[-1][...] = total.astype(BF16)


def home_body(count, *refs):
    mine, others = refs[:count], refs[count : 2 * count]
    state_ref, here_ref, there_ref, pick_ref, new_ref = refs[2 * count : 2 * count + 5]
    slots = jnp.concatenate([ref[...] for ref in mine], axis=0)
    far = jnp.concatenate([ref[...] for ref in others], axis=0)
    update = jnp.dot(here_ref[...], slots, preferred_element_type=F32)
    update = update + jnp.dot(there_ref[...], far, preferred_element_type=F32)
    state = (state_ref[...].astype(F32) + update).astype(BF16)
    new_ref[...] = state
    pack(state, pick_ref[...], refs[2 * count + 5 :])


def last_body(count, width, place_ref, *refs):
    core = place_ref[2]
    mine, others = refs[:count], refs[count : 2 * count]
    state_ref, here_ref, there_ref, out_ref = refs[2 * count :]
    columns = pl.ds(pl.multiple_of(core * width, width), width)
    slots = jnp.concatenate([ref[:, columns] for ref in mine], axis=0)
    far = jnp.concatenate([ref[:, columns] for ref in others], axis=0)
    update = jnp.dot(here_ref[...], slots, preferred_element_type=F32)
    update = update + jnp.dot(there_ref[...], far, preferred_element_type=F32)
    out_ref[...] = (state_ref[:, columns].astype(F32) + update).astype(BF16)


def shards(rows, path, norm_gain, gate_weight, up_weight, down_weight):
    local_rows, width = rows.shape
    hops = path.shape[0]
    ep_count, sub_count, tp_count = (lax.axis_size(a) for a in ("ep", "sub", "tp"))
    capacity = 2 * local_rows // (ep_count * tp_count)
    slots = ep_count * capacity
    half = width * tp_count
    features = half * sub_count
    hidden = gate_weight.shape[1]
    place = jnp.stack([lax.axis_index(a) for a in ("ep", "sub", "tp")]).astype(jnp.int32)
    weights = (norm_gain, gate_weight[0], up_weight[0], down_weight[0])
    relative = ep_count <= 4 and ep_count & (ep_count - 1) == 0
    count = ep_count if relative else 1
    height = slots // count
    piece = jax.ShapeDtypeStruct((height, half), BF16)
    whole = jax.ShapeDtypeStruct((local_rows, half), BF16)

    def across(value, s):
        if not relative:
            value = value.reshape(ep_count, capacity, half)
            return lax.all_to_all(value, "ep", 0, 0, tiled=True).reshape(slots, half)
        return value if s == 0 else swap(value, "ep", s)

    far = swap(rows, "tp", 1)
    square = (hops, local_rows, slots)
    here, there, pick = call(
        functools.partial(route_body, tp_count, capacity, relative),
        [jax.ShapeDtypeStruct(s, BF16) for s in (square, square, (hops, slots, local_rows))],
        place, path, scalars=1, name="route",
    )
    state, *pieces = call(
        functools.partial(first_body, width),
        [whole] + [piece] * count,
        place, rows, far, pick[0], scalars=1, name="first",
    )
    early = list(range((count + 1) // 2))
    late = list(range((count + 1) // 2, count))
    for hop in range(hops):
        arrived = {s: across(pieces[s], s) for s in late + early}
        full = {}
        for s in early + late:
            full[s] = [arrived[s]] + [swap(arrived[s], "sub", u) for u in range(1, sub_count)]
        back = {}
        for members in (early, late) if late else (early,):
            partial = call(
                functools.partial(expert_body, len(members), sub_count),
                [piece] * (len(members) * sub_count),
                place, *[p for s in members for p in full[s]], *weights,
                scalars=1, limit=16 << 20, name="expert",
                flops=6 * len(members) * height * hidden * features,
            )
            for i, s in enumerate(members):
                parts = partial[i * sub_count : (i + 1) * sub_count]
                parts = [parts[0]] + [swap(parts[u], "sub", u) for u in range(1, sub_count)]
                (back[s],) = call(sum_body, [piece], *parts, name="sum")
        mine = [across(back[s], s) for s in range(count)]
        others = [swap(m, "tp", 1) for m in mine]
        if hop + 1 < hops:
            state, *pieces = call(
                functools.partial(home_body, count),
                [whole] + [piece] * count,
                *mine, *others, state, here[hop], there[hop], pick[hop + 1], name="home",
            )
        else:
            (state,) = call(
                functools.partial(last_body, count, width),
                [jax.ShapeDtypeStruct(rows.shape, BF16)],
                place, *mine, *others, state, here[hop], there[hop], scalars=1, name="last",
            )
    return state


def solution(mesh):
    in_specs = (
        P(("groups", "ep"), ("sub", "tp")),
        P(None, ("groups", "ep"), None),
        P(("ep", "tp"), None),
        P(("ep", "tp"), "sub", None),
        P(("ep", "tp"), "sub", None),
        P(("ep", "tp"), "sub", None),
    )
    out_specs = P(("groups", "ep"), ("sub", "tp"))
    return jax.shard_map(shards, mesh=mesh, in_specs=in_specs, out_specs=out_specs, check_vma=False)
```

```python
import functools

import jax
import jax.numpy as jnp
from jax import lax
from jax.experimental import pallas as pl
from jax.experimental.pallas import tpu as pltpu
from jax.sharding import PartitionSpec as P

EPS = 1e-06
BF16 = jnp.bfloat16
F32 = jnp.float32
VMEM = pl.BlockSpec(memory_space=pltpu.VMEM)
SMEM = pl.BlockSpec(memory_space=pltpu.SMEM)


def call(body, outs, *operands, scalars=0, limit=12 << 20, scratch=(), flops=0):
    specs = [SMEM] * scalars + [VMEM] * (len(operands) - scalars)
    moved = sum(o.size * o.dtype.itemsize for o in operands) + sum(
        o.size * o.dtype.itemsize for o in outs
    )
    return pl.pallas_call(
        body,
        out_shape=outs,
        in_specs=specs,
        out_specs=[VMEM] * len(outs),
        scratch_shapes=list(scratch),
        compiler_params=pltpu.CompilerParams(vmem_limit_bytes=limit),
        cost_estimate=pl.CostEstimate(flops=flops, bytes_accessed=moved, transcendentals=0),
    )(*operands)


def swap(value, axis, step):
    return lax.ppermute(value, axis, [(i, i ^ step) for i in range(lax.axis_size(axis))])


def route_body(tp_count, capacity, relative, place_ref, path_ref, mine_ref, other_ref, pick_ref):
    ep_index, core_index = place_ref[0], place_ref[2]
    hops, local_rows, _ = path_ref.shape
    slots = mine_ref.shape[2]
    lane = lax.broadcasted_iota(jnp.int32, (local_rows, slots), 1)
    row = lax.broadcasted_iota(jnp.int32, (local_rows, local_rows), 0)
    col = lax.broadcasted_iota(jnp.int32, (local_rows, local_rows), 1)
    earlier = (col < row).astype(BF16)
    for hop in range(hops):
        expert = path_ref[hop]
        onehot = (expert == lane).astype(F32)
        before = jnp.dot(earlier, onehot.astype(BF16), preferred_element_type=F32)
        rank = jnp.sum(before * onehot, axis=1, keepdims=True).astype(jnp.int32)
        dest, core = lax.div(expert, tp_count), lax.rem(expert, tp_count)
        if relative:
            dest = lax.bitwise_xor(dest, ep_index)
        target = dest * capacity + rank
        here = jnp.where(core == core_index, target, -1) == lane
        there = jnp.where(core == core_index, -1, target) == lane
        mine_ref[hop] = here.astype(BF16)
        other_ref[hop] = there.astype(BF16)
        pick_ref[hop] = here.astype(F32).T.astype(BF16)


def first_body(width, place_ref, own_ref, far_ref, pick_ref, state_ref, *piece_refs):
    core = place_ref[2]
    state_ref[:, pl.ds(pl.multiple_of(core * width, width), width)] = own_ref[...]
    state_ref[:, pl.ds(pl.multiple_of((1 - core) * width, width), width)] = far_ref[...]
    pack(state_ref[...], pick_ref[...], piece_refs)


def pack(state, pick, piece_refs):
    height = piece_refs[0].shape[0]
    packed = jnp.dot(pick, state, preferred_element_type=F32).astype(BF16)
    for s, ref in enumerate(piece_refs):
        ref[...] = packed[s * height : (s + 1) * height]


def turn_body(block, weight_ref, out_ref):
    for b in range(weight_ref.shape[1] // block):
        out_ref[b * block : (b + 1) * block, :] = weight_ref[:, b * block : (b + 1) * block].T


def expert_body(count, sub_count, place_ref, *refs):
    x = place_ref[1]
    data = refs[: count * sub_count]
    gain_ref, gate_ref, up_ref, down_ref = refs[count * sub_count : count * sub_count + 4]
    out_refs = refs[count * sub_count + 4 :]
    width = data[0].shape[1]
    capacity = data[0].shape[0]
    total = 0.0
    values = []
    for u in range(sub_count):
        part = jnp.concatenate([data[i * sub_count + u][...] for i in range(count)], axis=0)
        part = part.astype(F32)
        values.append(part)
        total = total + jnp.sum(part * part, axis=-1, keepdims=True)
    scale = lax.rsqrt(total / (width * sub_count) + EPS)
    gate = up = 0.0
    for u in range(sub_count):
        columns = pl.ds(pl.multiple_of(lax.bitwise_xor(x, u) * width, width), width)
        normed = (values[u] * scale * gain_ref[:, columns]).astype(BF16)
        gate = gate + jnp.dot(normed, gate_ref[columns, :], preferred_element_type=F32)
        up = up + jnp.dot(normed, up_ref[columns, :], preferred_element_type=F32)
    hidden = (gate / (1.0 + jnp.exp(-gate)) * up).astype(BF16)
    for u in range(sub_count):
        columns = pl.ds(pl.multiple_of(lax.bitwise_xor(x, u) * width, width), width)
        partial = jnp.dot(hidden, down_ref[:, columns], preferred_element_type=F32).astype(BF16)
        for i in range(count):
            out_refs[i * sub_count + u][...] = partial[i * capacity : (i + 1) * capacity]


def sum_body(*refs):
    total = refs[0][...].astype(F32)
    for ref in refs[1:-1]:
        total = total + ref[...].astype(F32)
    refs[-1][...] = total.astype(BF16)


def home_body(count, *refs):
    mine, others = refs[:count], refs[count : 2 * count]
    state_ref, here_ref, there_ref, pick_ref, new_ref = refs[2 * count : 2 * count + 5]
    slots = jnp.concatenate([ref[...] for ref in mine], axis=0)
    far = jnp.concatenate([ref[...] for ref in others], axis=0)
    update = jnp.dot(here_ref[...], slots, preferred_element_type=F32)
    update = update + jnp.dot(there_ref[...], far, preferred_element_type=F32)
    state = (state_ref[...].astype(F32) + update).astype(BF16)
    new_ref[...] = state
    pack(state, pick_ref[...], refs[2 * count + 5 :])


def last_body(count, width, place_ref, *refs):
    core = place_ref[2]
    mine, others = refs[:count], refs[count : 2 * count]
    state_ref, here_ref, there_ref, out_ref = refs[2 * count :]
    columns = pl.ds(pl.multiple_of(core * width, width), width)
    slots = jnp.concatenate([ref[:, columns] for ref in mine], axis=0)
    far = jnp.concatenate([ref[:, columns] for ref in others], axis=0)
    update = jnp.dot(here_ref[...], slots, preferred_element_type=F32)
    update = update + jnp.dot(there_ref[...], far, preferred_element_type=F32)
    out_ref[...] = (state_ref[:, columns].astype(F32) + update).astype(BF16)


def shards(rows, path, norm_gain, gate_weight, up_weight, down_weight):
    local_rows, width = rows.shape
    hops = path.shape[0]
    ep_count, sub_count, tp_count = (lax.axis_size(a) for a in ("ep", "sub", "tp"))
    capacity = 2 * local_rows // (ep_count * tp_count)
    slots = ep_count * capacity
    half = width * tp_count
    features = half * sub_count
    hidden = gate_weight.shape[1]
    place = jnp.stack([lax.axis_index(a) for a in ("ep", "sub", "tp")]).astype(jnp.int32)
    relative = ep_count <= 4 and ep_count & (ep_count - 1) == 0
    count = ep_count if relative else 1
    height = slots // count
    piece = jax.ShapeDtypeStruct((height, half), BF16)
    whole = jax.ShapeDtypeStruct((local_rows, half), BF16)

    def across(value, s):
        if not relative:
            value = value.reshape(ep_count, capacity, half)
            return lax.all_to_all(value, "ep", 0, 0, tiled=True).reshape(slots, half)
        return value if s == 0 else swap(value, "ep", s)

    far = swap(rows, "tp", 1)
    square = (hops, local_rows, slots)
    here, there, pick = call(
        functools.partial(route_body, tp_count, capacity, relative),
        [jax.ShapeDtypeStruct(s, BF16) for s in (square, square, (hops, slots, local_rows))],
        place, path, scalars=1,
    )
    state, *pieces = call(
        functools.partial(first_body, width),
        [whole] + [piece] * count,
        place, rows, far, pick[0], scalars=1,
    )
    groups = ((2, 0), (3, 1)) if count == 4 else (tuple(range(count)),)
    order = [s for pair in zip(*groups) for s in pair]
    for hop in range(hops):
        if hop == 0:
            gate = turn(gate_weight[0])
            up = turn(up_weight[0])
            weights = (gate, up, down_weight[0])
        arrived, full, back = {}, {}, {}
        for s in order:
            arrived[s] = across(pieces[s], s)
        for s in order:
            full[s] = [arrived[s]] + [swap(arrived[s], "sub", u) for u in range(1, sub_count)]
        for members in groups:
            partial = call(
                functools.partial(expert_body, len(members), sub_count),
                [piece] * (len(members) * sub_count),
                place, *[p for s in members for p in full[s]], norm_gain, *weights,
                scalars=1, limit=16 << 20,
                flops=6 * len(members) * height * hidden * features,
            )
            for i, s in enumerate(members):
                parts = partial[i * sub_count : (i + 1) * sub_count]
                parts = [parts[0]] + [swap(parts[u], "sub", u) for u in range(1, sub_count)]
                (back[s],) = call(sum_body, [piece], *parts)
        mine, others = [], []
        for s in range(count):
            mine.append(across(back[s], s))
            others.append(swap(mine[s], "tp", 1))
        if hop + 1 < hops:
            state, *pieces = call(
                functools.partial(home_body, count),
                [whole] + [piece] * count,
                *mine, *others, state, here[hop], there[hop], pick[hop + 1],
            )
        else:
            (state,) = call(
                functools.partial(last_body, count, width),
                [jax.ShapeDtypeStruct(rows.shape, BF16)],
                place, *mine, *others, state, here[hop], there[hop], scalars=1,
            )
    return state


def turn(weight, block=512):
    out = jax.ShapeDtypeStruct(weight.shape[::-1], BF16)
    return call(functools.partial(turn_body, block), [out], weight)[0]


def solution(mesh):
    in_specs = (
        P(("groups", "ep"), ("sub", "tp")),
        P(None, ("groups", "ep"), None),
        P(("ep", "tp"), None),
        P(("ep", "tp"), "sub", None),
        P(("ep", "tp"), "sub", None),
        P(("ep", "tp"), "sub", None),
    )
    out_specs = P(("groups", "ep"), ("sub", "tp"))
    return jax.shard_map(shards, mesh=mesh, in_specs=in_specs, out_specs=out_specs, check_vma=False)
```

```python
import functools

import jax
import jax.numpy as jnp
from jax import lax
from jax.experimental import pallas as pl
from jax.experimental.pallas import tpu as pltpu
from jax.sharding import PartitionSpec as P

EPS = 1e-06
BF16 = jnp.bfloat16
F32 = jnp.float32
VMEM = pl.BlockSpec(memory_space=pltpu.VMEM)
SMEM = pl.BlockSpec(memory_space=pltpu.SMEM)


def call(body, outs, *operands, scalars=0, limit=12 << 20, scratch=(), flops=0):
    specs = [SMEM] * scalars + [VMEM] * (len(operands) - scalars)
    moved = sum(o.size * o.dtype.itemsize for o in operands) + sum(
        o.size * o.dtype.itemsize for o in outs
    )
    return pl.pallas_call(
        body,
        out_shape=outs,
        in_specs=specs,
        out_specs=[VMEM] * len(outs),
        scratch_shapes=list(scratch),
        compiler_params=pltpu.CompilerParams(vmem_limit_bytes=limit),
        cost_estimate=pl.CostEstimate(flops=flops, bytes_accessed=moved, transcendentals=0),
    )(*operands)


def swap(value, axis, step):
    return lax.ppermute(value, axis, [(i, i ^ step) for i in range(lax.axis_size(axis))])


def route_body(tp_count, capacity, relative, place_ref, path_ref, mine_ref, other_ref, pick_ref):
    ep_index, core_index = place_ref[0], place_ref[2]
    hops, local_rows = path_ref.shape
    slots = mine_ref.shape[2]
    lane = lax.broadcasted_iota(jnp.int32, (local_rows, slots), 1)
    row = lax.broadcasted_iota(jnp.int32, (local_rows, local_rows), 0)
    col = lax.broadcasted_iota(jnp.int32, (local_rows, local_rows), 1)
    earlier = (col < row).astype(BF16)
    for hop in range(hops):
        expert = jnp.broadcast_to(path_ref[hop : hop + 1], (local_rows, local_rows))
        expert = expert.astype(F32).T.astype(jnp.int32)[:, :1]
        onehot = (expert == lane).astype(F32)
        before = jnp.dot(earlier, onehot.astype(BF16), preferred_element_type=F32)
        rank = jnp.sum(before * onehot, axis=1, keepdims=True).astype(jnp.int32)
        dest, core = lax.div(expert, tp_count), lax.rem(expert, tp_count)
        if relative:
            dest = lax.bitwise_xor(dest, ep_index)
        target = dest * capacity + rank
        here = jnp.where(core == core_index, target, -1) == lane
        there = jnp.where(core == core_index, -1, target) == lane
        mine_ref[hop] = here.astype(BF16)
        other_ref[hop] = there.astype(BF16)
        pick_ref[hop] = here.astype(F32).T.astype(BF16)


def first_body(width, place_ref, own_ref, far_ref, pick_ref, state_ref, *piece_refs):
    core = place_ref[2]
    state_ref[:, pl.ds(pl.multiple_of(core * width, width), width)] = own_ref[...]
    state_ref[:, pl.ds(pl.multiple_of((1 - core) * width, width), width)] = far_ref[...]
    pack(state_ref[...], pick_ref[...], piece_refs)


def pack(state, pick, piece_refs):
    height = piece_refs[0].shape[0]
    packed = jnp.dot(pick, state, preferred_element_type=F32).astype(BF16)
    for s, ref in enumerate(piece_refs):
        ref[...] = packed[s * height : (s + 1) * height]


def turn_body(block, weight_ref, out_ref):
    for b in range(weight_ref.shape[1] // block):
        out_ref[b * block : (b + 1) * block, :] = weight_ref[:, b * block : (b + 1) * block].T


def expert_body(count, sub_count, place_ref, *refs):
    x = place_ref[1]
    data = refs[: count * sub_count]
    gain_ref, gate_ref, up_ref, down_ref = refs[count * sub_count : count * sub_count + 4]
    out_refs = refs[count * sub_count + 4 :]
    width = data[0].shape[1]
    capacity = data[0].shape[0]
    rows = count * capacity
    blank = [jnp.zeros((128 - rows, width), BF16)] if rows < 128 else []
    total = 0.0
    scaled, columns = [], []
    for u in range(sub_count):
        part = [data[i * sub_count + u][...] for i in range(count)] + blank
        part = jnp.concatenate(part, axis=0).astype(F32)
        total = total + jnp.sum(part * part, axis=-1, keepdims=True)
        columns.append(pl.ds(pl.multiple_of(lax.bitwise_xor(x, u) * width, width), width))
        scaled.append((part * gain_ref[:, columns[u]]).astype(BF16))
    scale = lax.rsqrt(total / (width * sub_count) + EPS)
    gate = up = 0.0
    for u in range(sub_count):
        gate = gate + jnp.dot(scaled[u], gate_ref[columns[u], :], preferred_element_type=F32)
        up = up + jnp.dot(scaled[u], up_ref[columns[u], :], preferred_element_type=F32)
    gate, up = gate * scale, up * scale
    hidden = (gate / (1.0 + jnp.exp(-gate)) * up).astype(BF16)
    for u in range(sub_count):
        partial = jnp.dot(hidden, down_ref[:, columns[u]], preferred_element_type=F32).astype(BF16)
        for i in range(count):
            out_refs[i * sub_count + u][...] = partial[i * capacity : (i + 1) * capacity]


def sum_body(*refs):
    total = refs[0][...].astype(F32)
    for ref in refs[1:-1]:
        total = total + ref[...].astype(F32)
    refs[-1][...] = total.astype(BF16)


def home_body(count, *refs):
    mine, others = refs[:count], refs[count : 2 * count]
    state_ref, here_ref, there_ref, pick_ref, new_ref = refs[2 * count : 2 * count + 5]
    slots = jnp.concatenate([ref[...] for ref in mine], axis=0)
    far = jnp.concatenate([ref[...] for ref in others], axis=0)
    update = jnp.dot(here_ref[...], slots, preferred_element_type=F32)
    update = update + jnp.dot(there_ref[...], far, preferred_element_type=F32)
    state = (state_ref[...].astype(F32) + update).astype(BF16)
    new_ref[...] = state
    pack(state, pick_ref[...], refs[2 * count + 5 :])


def last_body(count, width, place_ref, *refs):
    core = place_ref[2]
    mine, others = refs[:count], refs[count : 2 * count]
    state_ref, here_ref, there_ref, out_ref = refs[2 * count :]
    columns = pl.ds(pl.multiple_of(core * width, width), width)
    slots = jnp.concatenate([ref[:, columns] for ref in mine], axis=0)
    far = jnp.concatenate([ref[:, columns] for ref in others], axis=0)
    update = jnp.dot(here_ref[...], slots, preferred_element_type=F32)
    update = update + jnp.dot(there_ref[...], far, preferred_element_type=F32)
    out_ref[...] = (state_ref[:, columns].astype(F32) + update).astype(BF16)


def shards(rows, path, norm_gain, gate_weight, up_weight, down_weight):
    local_rows, width = rows.shape
    hops = path.shape[0]
    ep_count, sub_count, tp_count = (lax.axis_size(a) for a in ("ep", "sub", "tp"))
    capacity = 2 * local_rows // (ep_count * tp_count)
    slots = ep_count * capacity
    half = width * tp_count
    features = half * sub_count
    hidden = gate_weight.shape[1]
    place = jnp.stack([lax.axis_index(a) for a in ("ep", "sub", "tp")]).astype(jnp.int32)
    relative = ep_count <= 4 and ep_count & (ep_count - 1) == 0
    count = ep_count if relative else 1
    height = slots // count
    piece = jax.ShapeDtypeStruct((height, half), BF16)
    whole = jax.ShapeDtypeStruct((local_rows, half), BF16)

    def across(value, s):
        if not relative:
            value = value.reshape(ep_count, capacity, half)
            return lax.all_to_all(value, "ep", 0, 0, tiled=True).reshape(slots, half)
        return value if s == 0 else swap(value, "ep", s)

    far = swap(rows, "tp", 1)
    path = path.reshape(hops, local_rows)

    def route(first, last):
        square = (last - first, local_rows, slots)
        return call(
            functools.partial(route_body, tp_count, capacity, relative),
            [jax.ShapeDtypeStruct(s, BF16) for s in (square, square, (last - first, slots, local_rows))],
            place, path[first:last], scalars=1, flops=1 << 31,
        )

    routes = [[m[0] for m in route(0, 1)]]
    state, *pieces = call(
        functools.partial(first_body, width),
        [whole] + [piece] * count,
        place, rows, far, routes[0][2], scalars=1,
    )
    groups = ((2, 0), (3, 1)) if count == 4 else (tuple(range(count)),)
    order = list(range(count))
    for hop in range(hops):
        if hop == 0:
            later = route(1, hops)
            routes += [[m[i] for m in later] for i in range(hops - 1)]
            gate = turn(gate_weight[0])
            up = turn(up_weight[0])
            weights = (gate, up, down_weight[0])
        arrived, full, back = {}, {}, {}
        for s in order:
            arrived[s] = across(pieces[s], s)
        for s in order:
            full[s] = [arrived[s]] + [swap(arrived[s], "sub", u) for u in range(1, sub_count)]
        for members in groups:
            partial = call(
                functools.partial(expert_body, len(members), sub_count),
                [piece] * (len(members) * sub_count),
                place, *[p for s in members for p in full[s]], norm_gain, *weights,
                scalars=1, limit=16 << 20,
                flops=6 * len(members) * height * hidden * features,
            )
            for i, s in enumerate(members):
                parts = partial[i * sub_count : (i + 1) * sub_count]
                parts = [parts[0]] + [swap(parts[u], "sub", u) for u in range(1, sub_count)]
                (back[s],) = call(sum_body, [piece], *parts)
        mine, others = [], []
        for s in range(count):
            mine.append(across(back[s], s))
            others.append(swap(mine[s], "tp", 1))
        if hop + 1 < hops:
            state, *pieces = call(
                functools.partial(home_body, count),
                [whole] + [piece] * count,
                *mine, *others, state, *routes[hop][:2], routes[hop + 1][2],
            )
        else:
            (state,) = call(
                functools.partial(last_body, count, width),
                [jax.ShapeDtypeStruct(rows.shape, BF16)],
                place, *mine, *others, state, *routes[hop][:2], scalars=1,
            )
    return state


def turn(weight, block=512):
    out = jax.ShapeDtypeStruct(weight.shape[::-1], BF16)
    return call(functools.partial(turn_body, block), [out], weight)[0]


def solution(mesh):
    in_specs = (
        P(("groups", "ep"), ("sub", "tp")),
        P(None, ("groups", "ep"), None),
        P(("ep", "tp"), None),
        P(("ep", "tp"), "sub", None),
        P(("ep", "tp"), "sub", None),
        P(("ep", "tp"), "sub", None),
    )
    out_specs = P(("groups", "ep"), ("sub", "tp"))
    return jax.shard_map(shards, mesh=mesh, in_specs=in_specs, out_specs=out_specs, check_vma=False)
```
